32 devices in a mesh: region: 16 (over z, x, core), sub: 2 (over y).
Axes of the slice: x: 2, y: 2, z: 4, core: 2. Of those that a mesh axis runs over, the one named last changes fastest.
Arguments:
- source: float32 [8, 8, 8, 8192], P(None, None, None, ('region', 'sub')), may hold values from -3.5 to 4.5
- metric: float32 [3, 8, 8, 8, 8192], P(None, None, None, None, ('region', 'sub')), may hold values from 0.002 to 0.008
- face_area: float32 [6, 8192], P(None, ('region', 'sub')), may hold values from 0.5 to 13.5
- outlet_gain: float32 [8], replicated, may hold values from 0.0018310547 to 0.0073242188
- neighbour: int32 [6, 8192], P(None, ('region', 'sub')), may hold values from 0 to 2048, as said below
- orient: int32 [6, 8192], P(None, ('region', 'sub')), may hold values from 0 to 7
- outlet: int32 [6, 8192], P(None, ('region', 'sub')), may hold values from 0 to 8, as said below
- export_list: int32 [128, 128], P(('region', 'sub')), may hold values from 0 to 1535, as said below
Outputs:
- solution: float32 [8, 8, 8, 8192], P(None, None, None, ('region', 'sub'))
- residual: float32 [8, 8, 8, 8192], P(None, None, None, ('region', 'sub'))
The draws below stay inside these ranges and needn't reach their ends.
Inputs may be any that keep to these rules, and one draw needn't show every extreme that they name: Values below 1536 name the device's own faces, the next 128 each the four received lists in pool order; 2048 means the face has no neighbour, as on every outlet face and for any list from a device outside the mesh. 8 means the face belongs to no outlet. `export_list`: each row holds 128 different local face numbers.
All inputs are finite; a program needn't handle non-finite values.
Results may differ from the reference program's by a relative error of at most 0.0001.
Values sent between devices are 32-bit elements; how exact they have to be, the bound alone decides.
A program may use at most 64 MiB of HBM per device.

```python
import math
import jax
import jax.numpy as jnp
import numpy as np
from jax import lax

NP = 8
E_DEV = 256
OUTLETS = 8
ITERS = 4
SEND = 128
ELEMS = 8192
POOL = 2048
N_REGION = 16
N_SUB = 2
DEVICES = 32


def face_links(key):
    base = jax.random.fold_in(key, 17)
    keys = jax.random.split(base, 4)
    shape = (6, ELEMS)
    kind = jax.random.randint(keys[0], shape, 0, 8)
    own_pick = jax.random.randint(keys[1], shape, 0, 6 * E_DEV)
    slot_pick = jax.random.randint(keys[2], shape, 0, SEND)
    outlet_code = jax.random.randint(keys[3], shape, 0, 64)
    device = jnp.arange(ELEMS, dtype=jnp.int32) // E_DEV
    region_index = (device // N_SUB)[None, :]
    sub_index = (device % N_SUB)[None, :]
    present = jnp.where(kind == 4, sub_index > 0, jnp.where(kind == 5, sub_index < N_SUB - 1, jnp.where(kind == 6, region_index > 0, region_index < N_REGION - 1)))
    remote = 6 * E_DEV + (kind - 4) * SEND + slot_pick
    links = jnp.where(kind < 4, own_pick, jnp.where(present, remote, POOL))
    outlet_ids = jnp.where(outlet_code < OUTLETS, outlet_code, OUTLETS)
    links = jnp.where(outlet_ids < OUTLETS, POOL, links)
    return (links.astype(jnp.int32), outlet_ids.astype(jnp.int32))


def draw_neighbour(key, part):
    return face_links(key)[0]


def draw_outlet(key, part):
    return face_links(key)[1]


def draw_export_list(key, part):
    keys = jax.random.split(jax.random.fold_in(key, 29), 4 * DEVICES)
    picks = jax.vmap(lambda row_key: jax.random.permutation(row_key, 6 * E_DEV)[:SEND])(keys)
    return picks.astype(jnp.int32)


def draw_face_area(key, part):
    position = jnp.arange(ELEMS, dtype=jnp.float32) / max(ELEMS - 1, 1)
    spread = jax.random.uniform(key, (6, ELEMS), jnp.float32, jnp.log(0.5), jnp.log(1.5))
    return jnp.exp(spread) * (1.0 + 2.0 * position)[None, :]


def draw_source(key, part):
    shape = (NP, NP, NP, ELEMS)
    return jnp.clip(jax.random.normal(key, shape, jnp.float32), -4.0, 4.0) + 0.5


def touch_ends(drawn, key, smallest, high):
    place = [jax.random.randint(jax.random.fold_in(key, axis), (), 0, length) for axis, length in enumerate(drawn.shape)]
    main_axis = drawn.shape.index(max(drawn.shape))
    next_to = place[:main_axis] + [(place[main_axis] + 1) % drawn.shape[main_axis]] + place[main_axis + 1:]
    return drawn.at[tuple(place)].set(smallest).at[tuple(next_to)].set(high)


def block_levels(own_key, extent, shards, least, high):
    def one(axis_at, shards_of):
        heights = jax.random.uniform(jax.random.fold_in(jax.random.fold_in(own_key, 6), axis_at), (shards_of,), jnp.float32, least / len(shards), high / len(shards))
        return jnp.repeat(jnp.exp(heights), extent[axis_at] // shards_of).reshape((-1,) + (1,) * (len(extent) - axis_at - 1))

    loudness = one(*shards[0])
    for cut in shards[1:]:
        loudness = loudness * one(*cut)
    return loudness


def setup_inputs(seed: int = 0) -> dict:
    arg_keys = jax.random.split(jax.random.key(seed), 9)
    return {
        "source": draw_source(jax.random.fold_in(arg_keys[8], 71), 0),
        "metric": jnp.clip(jnp.exp(math.log(0.008) - 1.3862944 * jax.random.uniform(arg_keys[1], (3, NP, NP, NP, ELEMS), jnp.float32) ** block_levels(arg_keys[1], (3, NP, NP, NP, ELEMS), ((4, 32),), -0.2, 0.2)), 0.002, 0.008),
        "face_area": draw_face_area(jax.random.fold_in(arg_keys[8], 71), 0),
        "outlet_gain": jnp.clip(jnp.exp(jax.random.uniform(arg_keys[3], (OUTLETS,), jnp.float32, math.log(0.0018310547), math.log(0.0073242188))), 0.0018310547, 0.0073242188),
        "neighbour": draw_neighbour(jax.random.fold_in(arg_keys[8], 71), 0),
        "orient": touch_ends(jax.random.randint(arg_keys[5], (6, ELEMS), 0, 8), jax.random.fold_in(arg_keys[5], 1), 0, 7).astype(jnp.int32),
        "outlet": draw_outlet(jax.random.fold_in(arg_keys[8], 71), 0),
        "export_list": draw_export_list(jax.random.fold_in(arg_keys[8], 71), 0),
    }


GLL_POINTS = np.array([-1.0, -0.8717401485096066, -0.5917001814331423, -0.2092992179024789, 0.2092992179024789, 0.5917001814331423, 0.8717401485096066, 1.0])


def legendre_seven(points):
    previous = points * 0.0 + 1.0
    current = points * 1.0
    for degree in range(1, 7):
        previous, current = current, ((2 * degree + 1) * points * current - degree * previous) / (degree + 1)
    return current


def node_tables():
    values = legendre_seven(GLL_POINTS)
    weights = 2.0 / (56.0 * values * values)
    equal = (GLL_POINTS[:, None] == GLL_POINTS[None, :]) * 1.0
    differ = GLL_POINTS[:, None] - GLL_POINTS[None, :] + equal
    deriv = values[:, None] / (values[None, :] * differ) * (1.0 - equal)
    deriv[0, 0] = -14.0
    deriv[7, 7] = 14.0
    return deriv, np.outer(weights, weights).reshape(-1)


def stiffness(field, metric, deriv):
    highest = lax.Precision.HIGHEST
    grad_a = jnp.einsum('ai,ijke->ajke', deriv, field, precision=highest)
    grad_b = jnp.einsum('bj,ijke->ibke', deriv, field, precision=highest)
    grad_c = jnp.einsum('ck,ijke->ijce', deriv, field, precision=highest)
    result = jnp.einsum('ai,ajke->ijke', deriv, metric[0] * grad_a, precision=highest)
    result = result + jnp.einsum('bj,ibke->ijke', deriv, metric[1] * grad_b, precision=highest)
    return result + jnp.einsum('ck,ijce->ijke', deriv, metric[2] * grad_c, precision=highest)


def local_diagonal(metric, deriv):
    highest = lax.Precision.HIGHEST
    square = deriv * deriv
    result = jnp.einsum('ai,ajke->ijke', square, metric[0], precision=highest)
    result = result + jnp.einsum('bj,ibke->ijke', square, metric[1], precision=highest)
    return result + jnp.einsum('ck,ijce->ijke', square, metric[2], precision=highest)


def face_planes(field):
    return [field[0], field[NP - 1], field[:, 0], field[:, NP - 1], field[:, :, 0], field[:, :, NP - 1]]


def add_planes(field, pieces):
    field = field.at[0].add(pieces[0])
    field = field.at[NP - 1].add(pieces[1])
    field = field.at[:, 0].add(pieces[2])
    field = field.at[:, NP - 1].add(pieces[3])
    field = field.at[:, :, 0].add(pieces[4])
    return field.at[:, :, NP - 1].add(pieces[5])


def orient_blocks(grid, codes):
    result = jnp.zeros_like(grid)
    for variant in range(8):
        moved = grid
        if variant & 1:
            moved = jnp.flip(moved, axis=1)
        if variant & 2:
            moved = jnp.flip(moved, axis=2)
        if variant & 4:
            moved = jnp.swapaxes(moved, 1, 2)
        result = jnp.where(codes == variant, moved, result)
    return result


def assemble(values, neighbour, orient, export_list):
    devices = N_REGION * N_SUB
    stacked = jnp.stack(face_planes(values), axis=0).reshape(6, NP * NP, devices, E_DEV)
    own_faces = jnp.transpose(stacked, (2, 1, 0, 3)).reshape(devices, NP * NP, 6 * E_DEV)
    rows = export_list.reshape(devices, 4 * SEND)
    sent = jnp.take_along_axis(own_faces, rows[:, None, :], axis=2).reshape(N_REGION, N_SUB, NP * NP, 4, SEND)
    zero_sub = jnp.zeros((N_REGION, 1, NP * NP, SEND), values.dtype)
    zero_region = jnp.zeros((1, N_SUB, NP * NP, SEND), values.dtype)
    sub_low = jnp.concatenate([zero_sub, sent[:, :-1, :, 1]], axis=1)
    sub_high = jnp.concatenate([sent[:, 1:, :, 0], zero_sub], axis=1)
    region_low = jnp.concatenate([zero_region, sent[:-1, :, :, 3]], axis=0)
    region_high = jnp.concatenate([sent[1:, :, :, 2], zero_region], axis=0)
    face_pool = jnp.concatenate([own_faces.reshape(N_REGION, N_SUB, NP * NP, 6 * E_DEV), sub_low, sub_high, region_low, region_high], axis=3).reshape(devices, NP * NP, POOL)
    links = jnp.transpose(neighbour.reshape(6, devices, E_DEV), (1, 0, 2)).reshape(devices, 6 * E_DEV)
    codes = jnp.transpose(orient.reshape(6, devices, E_DEV), (1, 0, 2)).reshape(devices, 6 * E_DEV)
    fetched = jnp.take_along_axis(face_pool, jnp.minimum(links, POOL - 1)[:, None, :], axis=2)
    fetched = jnp.where(links[:, None, :] < POOL, fetched, 0.0)
    turned = orient_blocks(fetched.reshape(devices, NP, NP, 6 * E_DEV), codes[:, None, None, :])
    turned = jnp.transpose(turned.reshape(devices, NP, NP, 6, E_DEV), (3, 1, 2, 0, 4)).reshape(6, NP, NP, ELEMS)
    return add_planes(values, [turned[index] for index in range(6)])


def outlet_term(values, direction, face_area, outlet_gain, outlet, weights):
    highest = lax.Precision.HIGHEST
    faces = jnp.stack(face_planes(direction), axis=0).reshape(6, NP * NP, ELEMS)
    sums = jnp.einsum('q,fqe->fe', weights, faces, precision=highest)
    codes = jnp.arange(OUTLETS, dtype=jnp.int32)
    outlet_hits = (outlet[None, :, :] == codes[:, None, None]).astype(values.dtype)
    flux = jnp.einsum('ofe,fe->o', outlet_hits, face_area * sums, precision=highest)
    coeff = jnp.einsum('o,ofe->fe', outlet_gain * flux, outlet_hits, precision=highest) * face_area
    extra = (weights[None, :, None] * coeff[:, None, :]).reshape(6, NP, NP, ELEMS)
    return add_planes(values, [extra[index] for index in range(6)])


def reference(source, metric, face_area, outlet_gain, neighbour, orient, outlet, export_list):
    deriv_np, weights_np = node_tables()
    deriv = jnp.asarray(deriv_np, jnp.float32)
    weights = jnp.asarray(weights_np, jnp.float32)
    diagonal = assemble(local_diagonal(metric, deriv), neighbour, orient, export_list)
    inverse = 1.0 / diagonal
    centre = 4.5
    half_width = 3.5
    ratio = centre / half_width
    rho_prev = 1.0 / ratio
    residual = source
    direction = inverse * residual / centre
    solution = jnp.zeros_like(source)
    for sweep in range(ITERS):
        solution = solution + direction
        image = assemble(stiffness(direction, metric, deriv), neighbour, orient, export_list)
        image = outlet_term(image, direction, face_area, outlet_gain, outlet, weights)
        residual = residual - image
        rho_next = 1.0 / (2.0 * ratio - rho_prev)
        direction = rho_next * rho_prev * direction + (2.0 * rho_next / half_width) * inverse * residual
        rho_prev = rho_next
    solution = solution + direction
    return solution, residual
```

```python
import functools

import jax
import jax.numpy as jnp
import numpy as np
from jax import lax
from jax.experimental import pallas as pl
from jax.experimental.pallas import tpu as pltpu
from jax.sharding import PartitionSpec as P

NP = 8
ITERS = 4
MESH = pl.DeviceIdType.MESH
F32 = jnp.float32
BF16 = jnp.bfloat16

GLL_POINTS = np.array(
    [
        -1.0,
        -0.8717401485096066,
        -0.5917001814331423,
        -0.2092992179024789,
        0.2092992179024789,
        0.5917001814331423,
        0.8717401485096066,
        1.0,
    ]
)


def legendre_seven(points):
    previous = points * 0.0 + 1.0
    current = points * 1.0
    for degree in range(1, 7):
        previous, current = (
            current,
            ((2 * degree + 1) * points * current - degree * previous) / (degree + 1),
        )
    return current


def node_tables():
    values = legendre_seven(GLL_POINTS)
    weights = 2.0 / (56.0 * values * values)
    equal = (GLL_POINTS[:, None] == GLL_POINTS[None, :]) * 1.0
    differ = GLL_POINTS[:, None] - GLL_POINTS[None, :] + equal
    deriv = values[:, None] / (values[None, :] * differ) * (1.0 - equal)
    deriv[0, 0] = -14.0
    deriv[7, 7] = 14.0
    return deriv, weights


DERIV, WEIGHTS = node_tables()
DERIV = DERIV.astype(np.float32).astype(np.float64)


def split_table(table):
    table = np.kron(np.eye(NP), table)
    high = table.astype(jnp.bfloat16).astype(np.float64)
    return np.concatenate([high, high, table - high], axis=1)


def turn_variants():
    grid = np.arange(NP * NP).reshape(NP, NP)
    forms = [grid, grid[:, ::-1], grid.T, grid.T[:, ::-1]]
    table = np.zeros((4 * NP * NP, NP * NP))
    for form, moved in enumerate(forms):
        for place, origin in enumerate(moved.reshape(-1)):
            table[form * NP * NP + place, origin] = 1.0
    return np.concatenate([table, table], axis=1)


def small_apply(table, parts, sign):
    half = NP // 2
    even = [parts[i] + parts[NP - 1 - i] for i in range(half)]
    odd = [parts[i] - parts[NP - 1 - i] for i in range(half)]
    out = [None] * NP
    for a in range(half):
        p = q = None
        for i in range(half):
            plus = float(0.5 * (table[a, i] + table[a, NP - 1 - i])) * even[i]
            minus = float(0.5 * (table[a, i] - table[a, NP - 1 - i])) * odd[i]
            p = plus if p is None else p + plus
            q = minus if q is None else q + minus
        out[a] = p + q
        out[NP - 1 - a] = p - q if sign > 0 else q - p
    return out


def split(x):
    high = x.astype(BF16)
    low = (x - high.astype(F32)).astype(BF16)
    return high, low


def along_k(table, x):
    high, low = split(x)
    return jnp.dot(table, jnp.concatenate([high, low, high], axis=0), preferred_element_type=F32)


def kernel(
    n_region,
    n_sub,
    source,
    metric,
    face_area,
    gain,
    neighbour,
    orient,
    outlet,
    export_list,
    tables,
    turner,
    sol,
    res,
    field,
    direction,
    inverse,
    pool,
    export_hot,
    link_hot,
    got,
    send_buf,
    recv_buf,
    sub_part,
    sub_recv,
    reg_part,
    reg_recv,
    ex_send,
    ex_recv,
    sub_send_sem,
    sub_recv_sem,
    reg_send_sem,
    reg_recv_sem,
):
    elems = source.shape[3]
    slots = export_list.shape[1]
    own = 6 * elems
    region = lax.axis_index("region")
    sub = lax.axis_index("sub")
    square = DERIV * DERIV

    recv_buf[...] = jnp.zeros_like(recv_buf)

    barrier = pltpu.get_barrier_semaphore()

    @pl.loop(1, n_region)
    def _(k):
        peer = lax.rem(region + k, n_region)
        pl.semaphore_signal(barrier, inc=1, device_id={"region": peer, "sub": sub}, device_id_type=MESH)

    @pl.loop(1, n_sub)
    def _(k):
        peer = lax.rem(sub + k, n_sub)
        pl.semaphore_signal(barrier, inc=1, device_id={"region": region, "sub": peer}, device_id_type=MESH)

    chunk = 64

    @pl.loop(0, own // chunk)
    def _(p):
        start = pl.multiple_of(p * chunk, chunk)
        rows = lax.broadcasted_iota(jnp.int32, (chunk, slots), 0) + start
        for r in range(4):
            hit = jnp.where(rows == export_list[r : r + 1, :], 1.0, 0.0)
            export_hot[pl.ds(start, chunk), r * slots : (r + 1) * slots] = hit.astype(BF16)

    def build_links():
        @pl.loop(0, link_hot.shape[1] // chunk)
        def _(p):
            start = pl.multiple_of(p * chunk, chunk)
            rows = lax.broadcasted_iota(jnp.int32, (chunk, elems), 0) + start
            for f in range(6):
                hit = jnp.where(rows == neighbour[f : f + 1, :], 1.0, 0.0)
                link_hot[f, pl.ds(start, chunk), :] = hit.astype(BF16)

    routes = (
        (1, sub < n_sub - 1, {"region": region, "sub": jnp.minimum(sub + 1, n_sub - 1)}, sub > 0),
        (0, sub > 0, {"region": region, "sub": jnp.maximum(sub - 1, 0)}, sub < n_sub - 1),
        (3, region < n_region - 1, {"region": jnp.minimum(region + 1, n_region - 1), "sub": sub}, region > 0),
        (2, region > 0, {"region": jnp.maximum(region - 1, 0), "sub": sub}, region < n_region - 1),
    )

    def copy_of(turn, slot):
        row, _, peer, _ = routes[slot]
        return pltpu.make_async_remote_copy(
            src_ref=send_buf.at[turn, row],
            dst_ref=recv_buf.at[turn, slot],
            send_sem=ex_send.at[turn, slot],
            recv_sem=ex_recv.at[turn, slot],
            device_id=peer,
            device_id_type=MESH,
        )

    k_id = lax.broadcasted_iota(jnp.int32, (NP, elems), 0)
    lowest = k_id == 0
    highest = k_id == NP - 1

    def exchange(turn):
        def put(f, block):
            high, low = split(block)
            pool[0:64, f * elems : (f + 1) * elems] = high
            pool[64:128, f * elems : (f + 1) * elems] = low

        put(0, field[0].reshape(64, elems))
        put(1, field[NP - 1].reshape(64, elems))
        put(2, jnp.concatenate([field[i, 0] for i in range(NP)], axis=0))
        put(3, jnp.concatenate([field[i, NP - 1] for i in range(NP)], axis=0))
        for f, k in ((4, 0), (5, NP - 1)):
            rows = []
            for i in range(NP):
                block = jnp.broadcast_to(field[i, 0, k : k + 1, :], (NP, elems))
                for j in range(1, NP):
                    block = jnp.where(k_id == j, field[i, j, k : k + 1, :], block)
                rows.append(block)
            put(f, jnp.concatenate(rows, axis=0))
        both = jnp.dot(pool[...], export_hot[...], preferred_element_type=F32)
        sent = both[0:64] + both[64:128]
        for r in range(4):
            send_buf[turn, r] = sent[:, r * slots : (r + 1) * slots]
        for slot in range(4):

            @pl.when(routes[slot][1])
            def _(slot=slot):
                copy_of(turn, slot).start()

    def own_part():
        @pl.loop(0, 6)
        def _(f):
            got[f] = jnp.dot(pool[...], link_hot[f, 0:own, :], preferred_element_type=F32)

    def finish(turn, coeff):
        for slot in range(4):

            @pl.when(routes[slot][3])
            def _(slot=slot):
                copy_of(turn, slot).wait_recv()

            @pl.when(routes[slot][1])
            def _(slot=slot):
                copy_of(turn, slot).wait_send()

        arrived = jnp.concatenate([recv_buf[turn, s] for s in range(4)], axis=1)
        high, low = split(arrived)
        arrived = jnp.concatenate([high, low], axis=0)
        w_col = jnp.zeros((NP, elems), F32)
        for b in range(NP):
            w_col = jnp.where(k_id == b, float(WEIGHTS[b]), w_col)
        held = []
        for f in range(6):
            fetched = got[f] + jnp.dot(
                arrived, link_hot[f, own:, :], preferred_element_type=F32
            )
            forms = jnp.dot(turner[...], fetched.astype(BF16), preferred_element_type=F32)
            code = jnp.broadcast_to(orient[f : f + 1, :], (NP, elems))
            bit0 = (code & 1) == 1
            bit1 = (code & 2) == 2
            bit2 = (code & 4) == 4
            is_turned = bit2
            reversed_cols = ((code & 6) == 2) | ((code & 5) == 5)
            flip = ((code & 5) == 1) | ((code & 6) == 6)
            base = []
            for a in range(NP):
                form = [forms[m * 64 + a * NP : m * 64 + a * NP + NP] for m in range(4)]
                base.append(
                    jnp.where(
                        is_turned,
                        jnp.where(reversed_cols, form[3], form[2]),
                        jnp.where(reversed_cols, form[1], form[0]),
                    )
                )
            out = [jnp.where(flip, base[NP - 1 - a], base[a]) for a in range(NP)]
            if coeff is not None:
                spread = coeff[f] * w_col
                out = [out[a] + float(WEIGHTS[a]) * spread for a in range(NP)]
            if f < 2:
                for a in range(NP):
                    field[f * (NP - 1), a] += out[a]
            elif f < 4:
                for a in range(NP):
                    field[a, (f - 2) * (NP - 1)] += out[a]
            else:
                held.append(out)
        for a in range(NP):
            for j in range(NP):
                extra = jnp.where(
                    lowest,
                    held[0][a][j : j + 1, :],
                    jnp.where(highest, held[1][a][j : j + 1, :], 0.0),
                )
                field[a, j] += extra

    for t in range(NP):
        out = small_apply(square.T, [metric[0, a, t] for a in range(NP)], 1)
        for i in range(NP):
            field[i, t] = out[i]
    for t in range(NP):
        out = small_apply(square.T, [metric[1, t, b] for b in range(NP)], 1)
        along = along_k(tables[2], metric[2, t].reshape(64, elems)).reshape(NP, NP, elems)
        for j in range(NP):
            field[t, j] += out[j] + along[j]

    pl.semaphore_wait(barrier, n_region + n_sub - 2)

    exchange(0)
    build_links()
    own_part()
    finish(0, None)

    ratio = 4.5 / 3.5

    @pl.loop(0, NP)
    def _(t):
        inv = 1.0 / field[t]
        inverse[t] = inv
        first = inv * source[t] / 4.5
        direction[t] = first
        sol[t] = first
        res[t] = source[t]

    lanes = 128
    o_id = lax.broadcasted_iota(jnp.int32, (NP, elems), 0)
    diag = lax.broadcasted_iota(jnp.int32, (NP, lanes), 0) == lax.broadcasted_iota(
        jnp.int32, (NP, lanes), 1
    )

    def sub_copy(it, peer, owner):
        return pltpu.make_async_remote_copy(
            src_ref=sub_part.at[it],
            dst_ref=sub_recv.at[it, owner],
            send_sem=sub_send_sem.at[it, peer],
            recv_sem=sub_recv_sem.at[it, owner],
            device_id={"region": region, "sub": peer},
            device_id_type=MESH,
        )

    def reg_copy(it, peer, owner):
        return pltpu.make_async_remote_copy(
            src_ref=reg_part.at[it],
            dst_ref=reg_recv.at[it, owner],
            send_sem=reg_send_sem.at[it, peer],
            recv_sem=reg_recv_sem.at[it, owner],
            device_id={"region": peer, "sub": sub},
            device_id_type=MESH,
        )

    def flux_start(it):
        w_col = jnp.zeros((NP, elems), F32)
        for b in range(NP):
            w_col = jnp.where(k_id == b, float(WEIGHTS[b]), w_col)

        def line(parts):
            total = float(WEIGHTS[0]) * parts[0]
            for a in range(1, NP):
                total = total + float(WEIGHTS[a]) * parts[a]
            return total

        sums = []
        for i in (0, NP - 1):
            sums.append(line([direction[i, a] for a in range(NP)]))
        for j in (0, NP - 1):
            sums.append(line([direction[a, j] for a in range(NP)]))
        sums = [jnp.sum(s * w_col, axis=0, keepdims=True) for s in sums]
        whole = line([line([direction[i, j] for j in range(NP)]) for i in range(NP)])
        sums += [whole[0:1], whole[NP - 1 : NP]]
        total = jnp.zeros((NP, elems), F32)
        for f in range(6):
            part = face_area[f : f + 1, :] * sums[f]
            total = total + jnp.where(outlet[f : f + 1, :] == o_id, part, 0.0)
        column = jnp.sum(total, axis=1, keepdims=True)
        row = jnp.sum(jnp.where(diag, column, 0.0), axis=0, keepdims=True)
        sub_part[it] = row

        @pl.loop(1, n_sub)
        def _(k):
            peer = lax.rem(sub + k, n_sub)
            sub_copy(it, peer, sub).start()

    def flux_middle(it):
        def more(k, total):
            owner = lax.rem(sub + k, n_sub)
            sub_copy(it, owner, owner).wait()
            return total + sub_recv[it, owner]

        total = lax.fori_loop(1, n_sub, more, sub_part[it])
        reg_part[it] = total

        @pl.loop(1, n_region)
        def _(k):
            peer = lax.rem(region + k, n_region)
            reg_copy(it, peer, region).start()

    def flux_end(it):
        def more(k, total):
            owner = lax.rem(region + k, n_region)
            reg_copy(it, owner, owner).wait()
            return total + reg_recv[it, owner]

        row = lax.fori_loop(1, n_region, more, reg_part[it])
        scaled = row * gain[...]
        column = jnp.sum(
            jnp.where(diag, jnp.broadcast_to(scaled, (NP, lanes)), 0.0), axis=1, keepdims=True
        )
        coeff = []
        for f in range(6):
            picked = jnp.sum(
                jnp.where(outlet[f : f + 1, :] == o_id, column, 0.0), axis=0, keepdims=True
            )
            coeff.append(picked * face_area[f : f + 1, :])
        return coeff

    def stiffness():
        for t in range(NP):
            grads = small_apply(DERIV, [direction[i, t] for i in range(NP)], -1)
            grads = [grads[a] * metric[0, a, t] for a in range(NP)]
            out = small_apply(DERIV.T, grads, -1)
            for i in range(NP):
                field[i, t] = out[i]
        for t in range(NP):
            along = along_k(tables[0], direction[t].reshape(64, elems))
            along = along * metric[2, t].reshape(64, elems)
            along = along_k(tables[1], along).reshape(NP, NP, elems)
            grads = small_apply(DERIV, [direction[t, j] for j in range(NP)], -1)
            grads = [grads[b] * metric[1, t, b] for b in range(NP)]
            out = small_apply(DERIV.T, grads, -1)
            for j in range(NP):
                field[t, j] += out[j] + along[j]

    rho = 1.0 / ratio
    scales = []
    for it in range(ITERS):
        rho_next = 1.0 / (2.0 * ratio - rho)
        scales.append((rho_next * rho, 2.0 * rho_next / 3.5))
        rho = rho_next

    @pl.loop(0, ITERS)
    def _(it):
        keep, gain_now = (jnp.float32(scales[0][0]), jnp.float32(scales[0][1]))
        for step in range(1, ITERS):
            keep = jnp.where(it == step, jnp.float32(scales[step][0]), keep)
            gain_now = jnp.where(it == step, jnp.float32(scales[step][1]), gain_now)
        flux_start(it)
        stiffness()
        flux_middle(it)
        exchange(it + 1)
        own_part()
        finish(it + 1, flux_end(it))

        @pl.loop(0, NP)
        def _(t):
            left = res[t] - field[t]
            res[t] = left
            fresh = keep * direction[t] + gain_now * inverse[t] * left
            direction[t] = fresh
            sol[t] = sol[t] + fresh


def per_device(n_region, n_sub, source, metric, face_area, outlet_gain, neighbour, orient, outlet, export_list):
    elems = source.shape[3]
    slots = export_list.shape[1]
    own = 6 * elems
    full = own + 4 * slots
    outlets = outlet_gain.shape[0]
    gain = jnp.pad(outlet_gain.reshape(1, outlets), ((0, 0), (0, 128 - outlets)))
    square = DERIV * DERIV
    tables = jnp.asarray(
        np.stack([split_table(DERIV), split_table(DERIV.T), split_table(square.T)]), BF16
    )
    turner = jnp.asarray(turn_variants(), BF16)
    shape = jax.ShapeDtypeStruct(source.shape, F32)
    vmem = pl.BlockSpec(memory_space=pltpu.VMEM)
    dma = pltpu.SemaphoreType.DMA
    return pl.pallas_call(
        functools.partial(kernel, n_region, n_sub),
        out_shape=(shape, shape),
        in_specs=[vmem] * 10,
        out_specs=(vmem, vmem),
        scratch_shapes=[
            pltpu.VMEM(source.shape, F32),
            pltpu.VMEM(source.shape, F32),
            pltpu.VMEM(source.shape, F32),
            pltpu.VMEM((128, own), BF16),
            pltpu.VMEM((own, 4 * slots), BF16),
            pltpu.VMEM((6, full, elems), BF16),
            pltpu.VMEM((6, 128, elems), F32),
            pltpu.VMEM((ITERS + 1, 4, 64, slots), F32),
            pltpu.VMEM((ITERS + 1, 4, 64, slots), F32),
            pltpu.VMEM((ITERS, 1, 128), F32),
            pltpu.VMEM((ITERS, n_sub, 1, 128), F32),
            pltpu.VMEM((ITERS, 1, 128), F32),
            pltpu.VMEM((ITERS, n_region, 1, 128), F32),
            dma((ITERS + 1, 4)),
            dma((ITERS + 1, 4)),
            dma((ITERS, n_sub)),
            dma((ITERS, n_sub)),
            dma((ITERS, n_region)),
            dma((ITERS, n_region)),
        ],
        compiler_params=pltpu.CompilerParams(collective_id=0, has_side_effects=True),
    )(source, metric, face_area, gain, neighbour, orient, outlet, export_list, tables, turner)


def solution(mesh):
    placed = (
        P(None, None, None, ("region", "sub")),
        P(None, None, None, None, ("region", "sub")),
        P(None, ("region", "sub")),
        P(),
        P(None, ("region", "sub")),
        P(None, ("region", "sub")),
        P(None, ("region", "sub")),
        P(("region", "sub"), None),
    )
    field = P(None, None, None, ("region", "sub"))
    return jax.shard_map(
        functools.partial(per_device, mesh.shape["region"], mesh.shape["sub"]),
        mesh=mesh,
        in_specs=placed,
        out_specs=(field, field),
        check_vma=False,
    )
```

```python
import functools

import jax
import jax.numpy as jnp
import numpy as np
from jax import lax
from jax.experimental import pallas as pl
from jax.experimental.pallas import tpu as pltpu
from jax.sharding import PartitionSpec as P

NP = 8
ITERS = 4
MESH = pl.DeviceIdType.MESH
F32 = jnp.float32
BF16 = jnp.bfloat16

GLL_POINTS = np.array(
    [
        -1.0,
        -0.8717401485096066,
        -0.5917001814331423,
        -0.2092992179024789,
        0.2092992179024789,
        0.5917001814331423,
        0.8717401485096066,
        1.0,
    ]
)


def legendre_seven(points):
    previous = points * 0.0 + 1.0
    current = points * 1.0
    for degree in range(1, 7):
        previous, current = (
            current,
            ((2 * degree + 1) * points * current - degree * previous) / (degree + 1),
        )
    return current


def node_tables():
    values = legendre_seven(GLL_POINTS)
    weights = 2.0 / (56.0 * values * values)
    equal = (GLL_POINTS[:, None] == GLL_POINTS[None, :]) * 1.0
    differ = GLL_POINTS[:, None] - GLL_POINTS[None, :] + equal
    deriv = values[:, None] / (values[None, :] * differ) * (1.0 - equal)
    deriv[0, 0] = -14.0
    deriv[7, 7] = 14.0
    return deriv, weights


DERIV, WEIGHTS = node_tables()
DERIV = DERIV.astype(np.float32).astype(np.float64)


def split_table(table):
    table = np.kron(np.eye(NP), table)
    high = table.astype(jnp.bfloat16).astype(np.float64)
    return np.concatenate([high, high, table - high], axis=1)


def turn_variants():
    grid = np.arange(NP * NP).reshape(NP, NP)
    forms = [grid, grid[:, ::-1], grid.T, grid.T[:, ::-1]]
    table = np.zeros((4 * NP * NP, NP * NP))
    for form, moved in enumerate(forms):
        for place, origin in enumerate(moved.reshape(-1)):
            table[form * NP * NP + place, origin] = 1.0
    return np.concatenate([table, table], axis=1)


def small_apply(table, parts, sign):
    half = NP // 2
    even = [parts[i] + parts[NP - 1 - i] for i in range(half)]
    odd = [parts[i] - parts[NP - 1 - i] for i in range(half)]
    out = [None] * NP
    for a in range(half):
        p = q = None
        for i in range(half):
            plus = float(0.5 * (table[a, i] + table[a, NP - 1 - i])) * even[i]
            minus = float(0.5 * (table[a, i] - table[a, NP - 1 - i])) * odd[i]
            p = plus if p is None else p + plus
            q = minus if q is None else q + minus
        out[a] = p + q
        out[NP - 1 - a] = p - q if sign > 0 else q - p
    return out


def split(x):
    high = x.astype(BF16)
    low = (x - high.astype(F32)).astype(BF16)
    return high, low


def along_k(table, x):
    high, low = split(x)
    return jnp.dot(table, jnp.concatenate([high, low, high], axis=0), preferred_element_type=F32)


def kernel(
    n_region,
    n_sub,
    source_hbm,
    metric_hbm,
    face_area,
    gain,
    neighbour,
    orient,
    outlet,
    export_list,
    tables,
    turner,
    sol,
    res,
    metric,
    field,
    direction,
    inverse,
    pool,
    export_hot,
    link_hot,
    got,
    send_buf,
    recv_buf,
    flux_part,
    flux_recv,
    ex_send,
    ex_recv,
    flux_send_sem,
    flux_recv_sem,
    load_sem,
):
    elems = res.shape[3]
    slots = export_list.shape[1]
    own = 6 * elems
    region = lax.axis_index("region")
    sub = lax.axis_index("sub")
    square = DERIV * DERIV
    devices = n_region * n_sub
    me = region * n_sub + sub

    loads = [
        pltpu.make_async_copy(metric_hbm.at[0], metric.at[0], load_sem.at[0]),
        pltpu.make_async_copy(metric_hbm.at[1], metric.at[1], load_sem.at[1]),
        pltpu.make_async_copy(metric_hbm.at[2], metric.at[2], load_sem.at[2]),
        pltpu.make_async_copy(source_hbm, res, load_sem.at[3]),
    ]
    for load in loads:
        load.start()

    recv_buf[...] = jnp.zeros_like(recv_buf)

    barrier = pltpu.get_barrier_semaphore()

    def peer_at(k):
        peer = lax.rem(me + k, devices)
        return {"region": lax.div(peer, n_sub), "sub": lax.rem(peer, n_sub)}

    @pl.loop(1, devices)
    def _(k):
        pl.semaphore_signal(barrier, inc=1, device_id=peer_at(k), device_id_type=MESH)

    chunk = 64

    @pl.loop(0, own // chunk)
    def _(p):
        start = pl.multiple_of(p * chunk, chunk)
        rows = lax.broadcasted_iota(jnp.int32, (chunk, slots), 0) + start
        for r in range(4):
            hit = jnp.where(rows == export_list[r : r + 1, :], 1.0, 0.0)
            export_hot[pl.ds(start, chunk), r * slots : (r + 1) * slots] = hit.astype(BF16)

    def build_links():
        @pl.loop(0, link_hot.shape[1] // chunk)
        def _(p):
            start = pl.multiple_of(p * chunk, chunk)
            rows = lax.broadcasted_iota(jnp.int32, (chunk, elems), 0) + start
            for f in range(6):
                hit = jnp.where(rows == neighbour[f : f + 1, :], 1.0, 0.0)
                link_hot[f, pl.ds(start, chunk), :] = hit.astype(BF16)

    routes = (
        (1, sub < n_sub - 1, {"region": region, "sub": jnp.minimum(sub + 1, n_sub - 1)}, sub > 0),
        (0, sub > 0, {"region": region, "sub": jnp.maximum(sub - 1, 0)}, sub < n_sub - 1),
        (3, region < n_region - 1, {"region": jnp.minimum(region + 1, n_region - 1), "sub": sub}, region > 0),
        (2, region > 0, {"region": jnp.maximum(region - 1, 0), "sub": sub}, region < n_region - 1),
    )

    def copy_of(turn, slot):
        row, _, peer, _ = routes[slot]
        return pltpu.make_async_remote_copy(
            src_ref=send_buf.at[turn, row],
            dst_ref=recv_buf.at[turn, slot],
            send_sem=ex_send.at[turn, slot],
            recv_sem=ex_recv.at[turn, slot],
            device_id=peer,
            device_id_type=MESH,
        )

    k_id = lax.broadcasted_iota(jnp.int32, (NP, elems), 0)
    lowest = k_id == 0
    highest = k_id == NP - 1

    def exchange(turn):
        def put(f, block):
            high, low = split(block)
            pool[0:64, f * elems : (f + 1) * elems] = high
            pool[64:128, f * elems : (f + 1) * elems] = low

        put(0, field[0].reshape(64, elems))
        put(1, field[NP - 1].reshape(64, elems))
        put(2, jnp.concatenate([field[i, 0] for i in range(NP)], axis=0))
        put(3, jnp.concatenate([field[i, NP - 1] for i in range(NP)], axis=0))
        for f, k in ((4, 0), (5, NP - 1)):
            rows = []
            for i in range(NP):
                block = jnp.broadcast_to(field[i, 0, k : k + 1, :], (NP, elems))
                for j in range(1, NP):
                    block = jnp.where(k_id == j, field[i, j, k : k + 1, :], block)
                rows.append(block)
            put(f, jnp.concatenate(rows, axis=0))
        both = jnp.dot(pool[...], export_hot[...], preferred_element_type=F32)
        sent = both[0:64] + both[64:128]
        for r in range(4):
            send_buf[turn, r] = sent[:, r * slots : (r + 1) * slots]
        for slot in range(4):

            @pl.when(routes[slot][1])
            def _(slot=slot):
                copy_of(turn, slot).start()

    def own_part():
        @pl.loop(0, 6)
        def _(f):
            got[f] = jnp.dot(pool[...], link_hot[f, 0:own, :], preferred_element_type=F32)

    def finish(turn):
        for slot in range(4):

            @pl.when(routes[slot][3])
            def _(slot=slot):
                copy_of(turn, slot).wait_recv()

            @pl.when(routes[slot][1])
            def _(slot=slot):
                copy_of(turn, slot).wait_send()

        arrived = jnp.concatenate([recv_buf[turn, s] for s in range(4)], axis=1)
        high, low = split(arrived)
        arrived = jnp.concatenate([high, low], axis=0)
        held = []
        for f in range(6):
            fetched = got[f] + jnp.dot(
                arrived, link_hot[f, own:, :], preferred_element_type=F32
            )
            forms = jnp.dot(turner[...], fetched.astype(BF16), preferred_element_type=F32)
            code = jnp.broadcast_to(orient[f : f + 1, :], (NP, elems))
            bit0 = (code & 1) == 1
            bit1 = (code & 2) == 2
            bit2 = (code & 4) == 4
            is_turned = bit2
            reversed_cols = ((code & 6) == 2) | ((code & 5) == 5)
            flip = ((code & 5) == 1) | ((code & 6) == 6)
            base = []
            for a in range(NP):
                form = [forms[m * 64 + a * NP : m * 64 + a * NP + NP] for m in range(4)]
                base.append(
                    jnp.where(
                        is_turned,
                        jnp.where(reversed_cols, form[3], form[2]),
                        jnp.where(reversed_cols, form[1], form[0]),
                    )
                )
            out = [jnp.where(flip, base[NP - 1 - a], base[a]) for a in range(NP)]
            if f < 2:
                for a in range(NP):
                    field[f * (NP - 1), a] += out[a]
            elif f < 4:
                for a in range(NP):
                    field[a, (f - 2) * (NP - 1)] += out[a]
            else:
                held.append(out)
        for a in range(NP):
            for j in range(NP):
                extra = jnp.where(
                    lowest,
                    held[0][a][j : j + 1, :],
                    jnp.where(highest, held[1][a][j : j + 1, :], 0.0),
                )
                field[a, j] += extra

    loads[0].wait()
    for t in range(NP):
        out = small_apply(square.T, [metric[0, a, t] for a in range(NP)], 1)
        for i in range(NP):
            field[i, t] = out[i]
    loads[1].wait()
    loads[2].wait()
    for t in range(NP):
        out = small_apply(square.T, [metric[1, t, b] for b in range(NP)], 1)
        along = along_k(tables[2], metric[2, t].reshape(64, elems)).reshape(NP, NP, elems)
        for j in range(NP):
            field[t, j] += out[j] + along[j]

    pl.semaphore_wait(barrier, devices - 1)

    exchange(0)
    build_links()
    own_part()
    finish(0)

    ratio = 4.5 / 3.5
    loads[3].wait()

    @pl.loop(0, NP)
    def _(t):
        inv = 1.0 / field[t]
        inverse[t] = inv
        first = inv * res[t] / 4.5
        direction[t] = first
        sol[t] = first

    lanes = 128
    o_id = lax.broadcasted_iota(jnp.int32, (NP, elems), 0)
    diag = lax.broadcasted_iota(jnp.int32, (NP, lanes), 0) == lax.broadcasted_iota(
        jnp.int32, (NP, lanes), 1
    )

    w_col = jnp.zeros((NP, elems), F32)
    for b in range(NP):
        w_col = jnp.where(k_id == b, float(WEIGHTS[b]), w_col)

    def flux_start(it):

        def line(parts):
            total = float(WEIGHTS[0]) * parts[0]
            for a in range(1, NP):
                total = total + float(WEIGHTS[a]) * parts[a]
            return total

        sums = []
        for i in (0, NP - 1):
            sums.append(line([direction[i, a] for a in range(NP)]))
        for j in (0, NP - 1):
            sums.append(line([direction[a, j] for a in range(NP)]))
        sums = [jnp.sum(s * w_col, axis=0, keepdims=True) for s in sums]
        whole = line([line([direction[i, j] for j in range(NP)]) for i in range(NP)])
        sums += [whole[0:1], whole[NP - 1 : NP]]
        total = jnp.zeros((NP, elems), F32)
        for f in range(6):
            part = face_area[f : f + 1, :] * sums[f]
            total = total + jnp.where(outlet[f : f + 1, :] == o_id, part, 0.0)
        column = jnp.sum(total, axis=1, keepdims=True)
        row = jnp.sum(jnp.where(diag, column, 0.0), axis=0, keepdims=True)
        flux_part[it] = row

        @pl.loop(1, devices)
        def _(k):
            pltpu.make_async_remote_copy(
                src_ref=flux_part.at[it],
                dst_ref=flux_recv.at[it, k - 1],
                send_sem=flux_send_sem.at[it],
                recv_sem=flux_recv_sem.at[it],
                device_id=peer_at(k),
                device_id_type=MESH,
            ).start()

    def flux_end(it):
        every = flux_recv.at[it]
        pltpu.make_async_copy(every, every, flux_recv_sem.at[it]).wait()
        pltpu.make_async_copy(every, every, flux_send_sem.at[it]).wait()
        row = flux_part[it] + jnp.sum(flux_recv[it], axis=0)
        column = jnp.sum(
            jnp.where(diag, jnp.broadcast_to(row, (NP, lanes)), 0.0), axis=1, keepdims=True
        )
        gains = jnp.zeros((NP, lanes), F32)
        g_id = lax.broadcasted_iota(jnp.int32, (NP, lanes), 0)
        for o in range(gain.shape[0]):
            gains = jnp.where(g_id == o, gain[o], gains)
        column = column * gains[:, 0:1]
        coeff = []
        for f in range(6):
            picked = jnp.sum(
                jnp.where(outlet[f : f + 1, :] == o_id, column, 0.0), axis=0, keepdims=True
            )
            coeff.append(picked * face_area[f : f + 1, :])
        return coeff

    def stiffness():
        for t in range(NP):
            grads = small_apply(DERIV, [direction[i, t] for i in range(NP)], -1)
            grads = [grads[a] * metric[0, a, t] for a in range(NP)]
            out = small_apply(DERIV.T, grads, -1)
            for i in range(NP):
                field[i, t] = out[i]
        for t in range(NP):
            along = along_k(tables[0], direction[t].reshape(64, elems))
            along = along * metric[2, t].reshape(64, elems)
            along = along_k(tables[1], along).reshape(NP, NP, elems)
            grads = small_apply(DERIV, [direction[t, j] for j in range(NP)], -1)
            grads = [grads[b] * metric[1, t, b] for b in range(NP)]
            out = small_apply(DERIV.T, grads, -1)
            for j in range(NP):
                field[t, j] += out[j] + along[j]

    rho = 1.0 / ratio
    scales = []
    for it in range(ITERS):
        rho_next = 1.0 / (2.0 * ratio - rho)
        scales.append((rho_next * rho, 2.0 * rho_next / 3.5))
        rho = rho_next

    @pl.loop(0, ITERS)
    def _(it):
        keep, gain_now = (jnp.float32(scales[0][0]), jnp.float32(scales[0][1]))
        for step in range(1, ITERS):
            keep = jnp.where(it == step, jnp.float32(scales[step][0]), keep)
            gain_now = jnp.where(it == step, jnp.float32(scales[step][1]), gain_now)
        flux_start(it)
        stiffness()
        exchange(it + 1)
        own_part()
        finish(it + 1)
        coeff = flux_end(it)
        ends = jnp.where(lowest, coeff[4], jnp.where(highest, coeff[5], 0.0))
        sides = [coeff[f] * w_col for f in range(4)]
        for i in range(NP):
            for j in range(NP):
                extra = float(WEIGHTS[i] * WEIGHTS[j]) * ends
                if i == 0:
                    extra = extra + float(WEIGHTS[j]) * sides[0]
                if i == NP - 1:
                    extra = extra + float(WEIGHTS[j]) * sides[1]
                if j == 0:
                    extra = extra + float(WEIGHTS[i]) * sides[2]
                if j == NP - 1:
                    extra = extra + float(WEIGHTS[i]) * sides[3]
                left = res[i, j] - field[i, j] - extra
                res[i, j] = left
                fresh = keep * direction[i, j] + gain_now * inverse[i, j] * left
                direction[i, j] = fresh
                sol[i, j] = sol[i, j] + fresh


def per_device(n_region, n_sub, source, metric, face_area, outlet_gain, neighbour, orient, outlet, export_list):
    elems = source.shape[3]
    slots = export_list.shape[1]
    own = 6 * elems
    full = own + 4 * slots
    square = DERIV * DERIV
    tables = jnp.asarray(
        np.stack([split_table(DERIV), split_table(DERIV.T), split_table(square.T)]), BF16
    )
    turner = jnp.asarray(turn_variants(), BF16)
    devices = n_region * n_sub
    vmem = pl.BlockSpec(memory_space=pltpu.VMEM)
    dma = pltpu.SemaphoreType.DMA
    smem = pl.BlockSpec(memory_space=pltpu.SMEM)
    anywhere = pl.BlockSpec(memory_space=pl.ANY)
    sol, res = pl.pallas_call(
        functools.partial(kernel, n_region, n_sub),
        out_shape=(pltpu.VMEM(source.shape, F32),) * 2,
        in_specs=[anywhere, anywhere, vmem, smem] + [vmem] * 6,
        out_specs=(vmem, vmem),
        scratch_shapes=[
            pltpu.VMEM(metric.shape, F32),
            pltpu.VMEM(source.shape, F32),
            pltpu.VMEM(source.shape, F32),
            pltpu.VMEM(source.shape, F32),
            pltpu.VMEM((128, own), BF16),
            pltpu.VMEM((own, 4 * slots), BF16),
            pltpu.VMEM((6, full, elems), BF16),
            pltpu.VMEM((6, 128, elems), F32),
            pltpu.VMEM((ITERS + 1, 4, 64, slots), F32),
            pltpu.VMEM((ITERS + 1, 4, 64, slots), F32),
            pltpu.VMEM((ITERS, 1, 128), F32),
            pltpu.VMEM((ITERS, devices - 1, 1, 128), F32),
            dma((ITERS + 1, 4)),
            dma((ITERS + 1, 4)),
            dma((ITERS,)),
            dma((ITERS,)),
            dma((4,)),
        ],
        compiler_params=pltpu.CompilerParams(collective_id=0, has_side_effects=True),
    )(source, metric, face_area, outlet_gain, neighbour, orient, outlet, export_list, tables, turner)
    shape = jax.ShapeDtypeStruct(source.shape, F32)
    return pl.pallas_call(
        write_out,
        out_shape=(shape, shape),
        in_specs=[anywhere, anywhere],
        out_specs=(anywhere, anywhere),
        scratch_shapes=[dma((2,))],
    )(pltpu.with_memory_space_constraint(sol, pltpu.VMEM), pltpu.with_memory_space_constraint(res, pltpu.VMEM))


def write_out(sol, res, sol_out, res_out, sems):
    copies = [
        pltpu.make_async_copy(sol, sol_out, sems.at[0]),
        pltpu.make_async_copy(res, res_out, sems.at[1]),
    ]
    for copy in copies:
        copy.start()
    for copy in copies:
        copy.wait()


def solution(mesh):
    placed = (
        P(None, None, None, ("region", "sub")),
        P(None, None, None, None, ("region", "sub")),
        P(None, ("region", "sub")),
        P(),
        P(None, ("region", "sub")),
        P(None, ("region", "sub")),
        P(None, ("region", "sub")),
        P(("region", "sub"), None),
    )
    field = P(None, None, None, ("region", "sub"))
    return jax.shard_map(
        functools.partial(per_device, mesh.shape["region"], mesh.shape["sub"]),
        mesh=mesh,
        in_specs=placed,
        out_specs=(field, field),
        check_vma=False,
    )
```

```python
import functools

import jax
import jax.numpy as jnp
import numpy as np
from jax import lax
from jax.experimental import pallas as pl
from jax.experimental.pallas import tpu as pltpu
from jax.sharding import PartitionSpec as P

NP = 8
ITERS = 4
MESH = pl.DeviceIdType.MESH
F32 = jnp.float32
BF16 = jnp.bfloat16

GLL_POINTS = np.array(
    [
        -1.0,
        -0.8717401485096066,
        -0.5917001814331423,
        -0.2092992179024789,
        0.2092992179024789,
        0.5917001814331423,
        0.8717401485096066,
        1.0,
    ]
)


def legendre_seven(points):
    previous = points * 0.0 + 1.0
    current = points * 1.0
    for degree in range(1, 7):
        previous, current = (
            current,
            ((2 * degree + 1) * points * current - degree * previous) / (degree + 1),
        )
    return current


def node_tables():
    values = legendre_seven(GLL_POINTS)
    weights = 2.0 / (56.0 * values * values)
    equal = (GLL_POINTS[:, None] == GLL_POINTS[None, :]) * 1.0
    differ = GLL_POINTS[:, None] - GLL_POINTS[None, :] + equal
    deriv = values[:, None] / (values[None, :] * differ) * (1.0 - equal)
    deriv[0, 0] = -14.0
    deriv[7, 7] = 14.0
    return deriv, weights


DERIV, WEIGHTS = node_tables()
DERIV = DERIV.astype(np.float32).astype(np.float64)


def split_table(table):
    table = np.kron(np.eye(NP), table)
    high = table.astype(jnp.bfloat16).astype(np.float64)
    return np.concatenate([high, high, table - high], axis=1)


def turn_variants():
    grid = np.arange(NP * NP).reshape(NP, NP)
    forms = [grid, grid[:, ::-1], grid.T, grid.T[:, ::-1]]
    table = np.zeros((4 * NP * NP, NP * NP))
    for form, moved in enumerate(forms):
        for place, origin in enumerate(moved.reshape(-1)):
            table[form * NP * NP + place, origin] = 1.0
    return np.concatenate([table, table], axis=1)


def small_apply(table, parts, sign):
    half = NP // 2
    even = [parts[i] + parts[NP - 1 - i] for i in range(half)]
    odd = [parts[i] - parts[NP - 1 - i] for i in range(half)]
    out = [None] * NP
    for a in range(half):
        p = q = None
        for i in range(half):
            plus = float(0.5 * (table[a, i] + table[a, NP - 1 - i])) * even[i]
            minus = float(0.5 * (table[a, i] - table[a, NP - 1 - i])) * odd[i]
            p = plus if p is None else p + plus
            q = minus if q is None else q + minus
        out[a] = p + q
        out[NP - 1 - a] = p - q if sign > 0 else q - p
    return out


def split(x):
    high = x.astype(BF16)
    low = (x - high.astype(F32)).astype(BF16)
    return high, low


def along_k(table, x):
    high, low = split(x)
    return jnp.dot(table, jnp.concatenate([high, low, high], axis=0), preferred_element_type=F32)


def kernel(
    n_region,
    n_sub,
    source_hbm,
    metric_hbm,
    face_area,
    gain,
    neighbour,
    orient,
    outlet,
    export_list,
    tables,
    turner,
    sol,
    res,
    metric,
    field,
    direction,
    inverse,
    pool,
    export_hot,
    link_hot,
    got,
    send_buf,
    recv_buf,
    flux_part,
    flux_recv,
    ex_send,
    ex_recv,
    flux_send_sem,
    flux_recv_sem,
    load_sem,
):
    elems = res.shape[3]
    slots = export_list.shape[1]
    own = 6 * elems
    region = lax.axis_index("region")
    sub = lax.axis_index("sub")
    square = DERIV * DERIV
    devices = n_region * n_sub

    loads = [
        pltpu.make_async_copy(metric_hbm.at[0], metric.at[0], load_sem.at[0]),
        pltpu.make_async_copy(metric_hbm.at[1], metric.at[1], load_sem.at[1]),
        pltpu.make_async_copy(metric_hbm.at[2], metric.at[2], load_sem.at[2]),
        pltpu.make_async_copy(source_hbm, res, load_sem.at[3]),
    ]
    for load in loads:
        load.start()

    recv_buf[...] = jnp.zeros_like(recv_buf)

    barrier = pltpu.get_barrier_semaphore()

    def wrapped(at, size):
        return jnp.where(at >= size, at - size, at)

    def every_peer(act):
        subs = [wrapped(sub + k, n_sub) for k in range(n_sub)]
        for k in range(1, n_sub):
            act(k - 1, {"region": region, "sub": subs[k]})

        @pl.loop(1, n_region)
        def _(step):
            there = wrapped(region + step, n_region)
            for k in range(n_sub):
                act(step * n_sub + k - 1, {"region": there, "sub": subs[k]})

    every_peer(
        lambda place, peer: pl.semaphore_signal(
            barrier, inc=1, device_id=peer, device_id_type=MESH
        )
    )

    chunk = 64

    @pl.loop(0, own // chunk)
    def _(p):
        start = pl.multiple_of(p * chunk, chunk)
        rows = lax.broadcasted_iota(jnp.int32, (chunk, slots), 0) + start
        for r in range(4):
            hit = jnp.where(rows == export_list[r : r + 1, :], 1.0, 0.0)
            export_hot[pl.ds(start, chunk), r * slots : (r + 1) * slots] = hit.astype(BF16)

    def build_links():
        @pl.loop(0, link_hot.shape[1] // chunk)
        def _(p):
            start = pl.multiple_of(p * chunk, chunk)
            rows = lax.broadcasted_iota(jnp.int32, (chunk, elems), 0) + start
            for f in range(6):
                hit = jnp.where(rows == neighbour[f : f + 1, :], 1.0, 0.0)
                link_hot[f, pl.ds(start, chunk), :] = hit.astype(BF16)

    routes = (
        (1, sub < n_sub - 1, {"region": region, "sub": jnp.minimum(sub + 1, n_sub - 1)}, sub > 0),
        (0, sub > 0, {"region": region, "sub": jnp.maximum(sub - 1, 0)}, sub < n_sub - 1),
        (3, region < n_region - 1, {"region": jnp.minimum(region + 1, n_region - 1), "sub": sub}, region > 0),
        (2, region > 0, {"region": jnp.maximum(region - 1, 0), "sub": sub}, region < n_region - 1),
    )

    def copy_of(turn, slot):
        row, _, peer, _ = routes[slot]
        return pltpu.make_async_remote_copy(
            src_ref=send_buf.at[turn, row],
            dst_ref=recv_buf.at[turn, slot],
            send_sem=ex_send.at[turn, slot],
            recv_sem=ex_recv.at[turn, slot],
            device_id=peer,
            device_id_type=MESH,
        )

    k_id = lax.broadcasted_iota(jnp.int32, (NP, elems), 0)
    lowest = k_id == 0
    highest = k_id == NP - 1

    def exchange(turn):
        def put(f, block):
            high, low = split(block)
            pool[0:64, f * elems : (f + 1) * elems] = high
            pool[64:128, f * elems : (f + 1) * elems] = low

        put(0, field[0].reshape(64, elems))
        put(1, field[NP - 1].reshape(64, elems))
        put(2, jnp.concatenate([field[i, 0] for i in range(NP)], axis=0))
        put(3, jnp.concatenate([field[i, NP - 1] for i in range(NP)], axis=0))
        for f, k in ((4, 0), (5, NP - 1)):
            rows = []
            for i in range(NP):
                block = jnp.broadcast_to(field[i, 0, k : k + 1, :], (NP, elems))
                for j in range(1, NP):
                    block = jnp.where(k_id == j, field[i, j, k : k + 1, :], block)
                rows.append(block)
            put(f, jnp.concatenate(rows, axis=0))
        both = jnp.dot(pool[...], export_hot[...], preferred_element_type=F32)
        sent = both[0:64] + both[64:128]
        for r in range(4):
            send_buf[turn, r] = sent[:, r * slots : (r + 1) * slots]
        for slot in range(4):

            @pl.when(routes[slot][1])
            def _(slot=slot):
                copy_of(turn, slot).start()

    def own_part():
        @pl.loop(0, 6)
        def _(f):
            got[f] = jnp.dot(pool[...], link_hot[f, 0:own, :], preferred_element_type=F32)

    def finish(turn):
        for slot in range(4):

            @pl.when(routes[slot][3])
            def _(slot=slot):
                copy_of(turn, slot).wait_recv()

            @pl.when(routes[slot][1])
            def _(slot=slot):
                copy_of(turn, slot).wait_send()

        arrived = jnp.concatenate([recv_buf[turn, s] for s in range(4)], axis=1)
        high, low = split(arrived)
        arrived = jnp.concatenate([high, low], axis=0)
        held = []
        for f in range(6):
            fetched = got[f] + jnp.dot(
                arrived, link_hot[f, own:, :], preferred_element_type=F32
            )
            forms = jnp.dot(turner[...], fetched.astype(BF16), preferred_element_type=F32)
            code = jnp.broadcast_to(orient[f : f + 1, :], (NP, elems))
            bit0 = (code & 1) == 1
            bit1 = (code & 2) == 2
            bit2 = (code & 4) == 4
            is_turned = bit2
            reversed_cols = ((code & 6) == 2) | ((code & 5) == 5)
            flip = ((code & 5) == 1) | ((code & 6) == 6)
            base = []
            for a in range(NP):
                form = [forms[m * 64 + a * NP : m * 64 + a * NP + NP] for m in range(4)]
                base.append(
                    jnp.where(
                        is_turned,
                        jnp.where(reversed_cols, form[3], form[2]),
                        jnp.where(reversed_cols, form[1], form[0]),
                    )
                )
            out = [jnp.where(flip, base[NP - 1 - a], base[a]) for a in range(NP)]
            if f < 2:
                for a in range(NP):
                    field[f * (NP - 1), a] += out[a]
            elif f < 4:
                for a in range(NP):
                    field[a, (f - 2) * (NP - 1)] += out[a]
            else:
                held.append(out)
        for a in range(NP):
            for j in range(NP):
                extra = jnp.where(
                    lowest,
                    held[0][a][j : j + 1, :],
                    jnp.where(highest, held[1][a][j : j + 1, :], 0.0),
                )
                field[a, j] += extra

    loads[0].wait()
    for t in range(NP):
        out = small_apply(square.T, [metric[0, a, t] for a in range(NP)], 1)
        for i in range(NP):
            field[i, t] = out[i]
    loads[1].wait()
    loads[2].wait()
    for t in range(NP):
        out = small_apply(square.T, [metric[1, t, b] for b in range(NP)], 1)
        along = along_k(tables[2], metric[2, t].reshape(64, elems)).reshape(NP, NP, elems)
        for j in range(NP):
            field[t, j] += out[j] + along[j]

    pl.semaphore_wait(barrier, devices - 1)

    exchange(0)
    build_links()
    own_part()
    finish(0)

    ratio = 4.5 / 3.5
    loads[3].wait()

    @pl.loop(0, NP)
    def _(t):
        inv = 1.0 / field[t]
        inverse[t] = inv
        first = inv * res[t] / 4.5
        direction[t] = first
        sol[t] = first

    lanes = 128
    o_id = lax.broadcasted_iota(jnp.int32, (NP, elems), 0)
    diag = lax.broadcasted_iota(jnp.int32, (NP, lanes), 0) == lax.broadcasted_iota(
        jnp.int32, (NP, lanes), 1
    )

    w_col = jnp.zeros((NP, elems), F32)
    for b in range(NP):
        w_col = jnp.where(k_id == b, float(WEIGHTS[b]), w_col)

    def flux_start(it):

        def line(parts):
            total = float(WEIGHTS[0]) * parts[0]
            for a in range(1, NP):
                total = total + float(WEIGHTS[a]) * parts[a]
            return total

        sums = []
        for i in (0, NP - 1):
            sums.append(line([direction[i, a] for a in range(NP)]))
        for j in (0, NP - 1):
            sums.append(line([direction[a, j] for a in range(NP)]))
        sums = [jnp.sum(s * w_col, axis=0, keepdims=True) for s in sums]
        whole = line([line([direction[i, j] for j in range(NP)]) for i in range(NP)])
        sums += [whole[0:1], whole[NP - 1 : NP]]
        total = jnp.zeros((NP, elems), F32)
        for f in range(6):
            part = face_area[f : f + 1, :] * sums[f]
            total = total + jnp.where(outlet[f : f + 1, :] == o_id, part, 0.0)
        column = jnp.sum(total, axis=1, keepdims=True)
        row = jnp.sum(jnp.where(diag, column, 0.0), axis=0, keepdims=True)
        flux_part[it] = row

        every_peer(
            lambda place, peer: pltpu.make_async_remote_copy(
                src_ref=flux_part.at[it],
                dst_ref=flux_recv.at[it, place],
                send_sem=flux_send_sem.at[it],
                recv_sem=flux_recv_sem.at[it],
                device_id=peer,
                device_id_type=MESH,
            ).start()
        )

    def flux_end(it):
        every = flux_recv.at[it]
        pltpu.make_async_copy(every, every, flux_recv_sem.at[it]).wait()
        pltpu.make_async_copy(every, every, flux_send_sem.at[it]).wait()
        row = flux_part[it] + jnp.sum(flux_recv[it], axis=0)
        column = jnp.sum(
            jnp.where(diag, jnp.broadcast_to(row, (NP, lanes)), 0.0), axis=1, keepdims=True
        )
        gains = jnp.zeros((NP, lanes), F32)
        g_id = lax.broadcasted_iota(jnp.int32, (NP, lanes), 0)
        for o in range(gain.shape[0]):
            gains = jnp.where(g_id == o, gain[o], gains)
        column = column * gains[:, 0:1]
        coeff = []
        for f in range(6):
            picked = jnp.sum(
                jnp.where(outlet[f : f + 1, :] == o_id, column, 0.0), axis=0, keepdims=True
            )
            coeff.append(picked * face_area[f : f + 1, :])
        return coeff

    def stiffness():
        for t in range(NP):
            grads = small_apply(DERIV, [direction[i, t] for i in range(NP)], -1)
            grads = [grads[a] * metric[0, a, t] for a in range(NP)]
            out = small_apply(DERIV.T, grads, -1)
            for i in range(NP):
                field[i, t] = out[i]
        for t in range(NP):
            along = along_k(tables[0], direction[t].reshape(64, elems))
            along = along * metric[2, t].reshape(64, elems)
            along = along_k(tables[1], along).reshape(NP, NP, elems)
            grads = small_apply(DERIV, [direction[t, j] for j in range(NP)], -1)
            grads = [grads[b] * metric[1, t, b] for b in range(NP)]
            out = small_apply(DERIV.T, grads, -1)
            for j in range(NP):
                field[t, j] += out[j] + along[j]

    rho = 1.0 / ratio
    scales = []
    for it in range(ITERS):
        rho_next = 1.0 / (2.0 * ratio - rho)
        scales.append((rho_next * rho, 2.0 * rho_next / 3.5))
        rho = rho_next

    @pl.loop(0, ITERS)
    def _(it):
        keep, gain_now = (jnp.float32(scales[0][0]), jnp.float32(scales[0][1]))
        for step in range(1, ITERS):
            keep = jnp.where(it == step, jnp.float32(scales[step][0]), keep)
            gain_now = jnp.where(it == step, jnp.float32(scales[step][1]), gain_now)
        flux_start(it)
        stiffness()
        exchange(it + 1)
        own_part()
        finish(it + 1)
        coeff = flux_end(it)
        ends = jnp.where(lowest, coeff[4], jnp.where(highest, coeff[5], 0.0))
        sides = [coeff[f] * w_col for f in range(4)]
        for i in range(NP):
            for j in range(NP):
                extra = float(WEIGHTS[i] * WEIGHTS[j]) * ends
                if i == 0:
                    extra = extra + float(WEIGHTS[j]) * sides[0]
                if i == NP - 1:
                    extra = extra + float(WEIGHTS[j]) * sides[1]
                if j == 0:
                    extra = extra + float(WEIGHTS[i]) * sides[2]
                if j == NP - 1:
                    extra = extra + float(WEIGHTS[i]) * sides[3]
                left = res[i, j] - field[i, j] - extra
                res[i, j] = left
                fresh = keep * direction[i, j] + gain_now * inverse[i, j] * left
                direction[i, j] = fresh
                sol[i, j] = sol[i, j] + fresh


def per_device(n_region, n_sub, source, metric, face_area, outlet_gain, neighbour, orient, outlet, export_list):
    elems = source.shape[3]
    slots = export_list.shape[1]
    own = 6 * elems
    full = own + 4 * slots
    square = DERIV * DERIV
    tables = jnp.asarray(
        np.stack([split_table(DERIV), split_table(DERIV.T), split_table(square.T)]), BF16
    )
    turner = jnp.asarray(turn_variants(), BF16)
    devices = n_region * n_sub
    vmem = pl.BlockSpec(memory_space=pltpu.VMEM)
    dma = pltpu.SemaphoreType.DMA
    smem = pl.BlockSpec(memory_space=pltpu.SMEM)
    anywhere = pl.BlockSpec(memory_space=pl.ANY)
    sol, res = pl.pallas_call(
        functools.partial(kernel, n_region, n_sub),
        out_shape=(pltpu.VMEM(source.shape, F32),) * 2,
        in_specs=[anywhere, anywhere, vmem, smem] + [vmem] * 6,
        out_specs=(vmem, vmem),
        scratch_shapes=[
            pltpu.VMEM(metric.shape, F32),
            pltpu.VMEM(source.shape, F32),
            pltpu.VMEM(source.shape, F32),
            pltpu.VMEM(source.shape, F32),
            pltpu.VMEM((128, own), BF16),
            pltpu.VMEM((own, 4 * slots), BF16),
            pltpu.VMEM((6, full, elems), BF16),
            pltpu.VMEM((6, 128, elems), F32),
            pltpu.VMEM((ITERS + 1, 4, 64, slots), F32),
            pltpu.VMEM((ITERS + 1, 4, 64, slots), F32),
            pltpu.VMEM((ITERS, 1, 128), F32),
            pltpu.VMEM((ITERS, devices - 1, 1, 128), F32),
            dma((ITERS + 1, 4)),
            dma((ITERS + 1, 4)),
            dma((ITERS,)),
            dma((ITERS,)),
            dma((4,)),
        ],
        compiler_params=pltpu.CompilerParams(collective_id=0, has_side_effects=True),
    )(source, metric, face_area, outlet_gain, neighbour, orient, outlet, export_list, tables, turner)
    shape = jax.ShapeDtypeStruct(source.shape, F32)
    return pl.pallas_call(
        write_out,
        out_shape=(shape, shape),
        in_specs=[anywhere, anywhere],
        out_specs=(anywhere, anywhere),
        scratch_shapes=[dma((2,))],
    )(pltpu.with_memory_space_constraint(sol, pltpu.VMEM), pltpu.with_memory_space_constraint(res, pltpu.VMEM))


def write_out(sol, res, sol_out, res_out, sems):
    copies = [
        pltpu.make_async_copy(sol, sol_out, sems.at[0]),
        pltpu.make_async_copy(res, res_out, sems.at[1]),
    ]
    for copy in copies:
        copy.start()
    for copy in copies:
        copy.wait()


def solution(mesh):
    placed = (
        P(None, None, None, ("region", "sub")),
        P(None, None, None, None, ("region", "sub")),
        P(None, ("region", "sub")),
        P(),
        P(None, ("region", "sub")),
        P(None, ("region", "sub")),
        P(None, ("region", "sub")),
        P(("region", "sub"), None),
    )
    field = P(None, None, None, ("region", "sub"))
    return jax.shard_map(
        functools.partial(per_device, mesh.shape["region"], mesh.shape["sub"]),
        mesh=mesh,
        in_specs=placed,
        out_specs=(field, field),
        check_vma=False,
    )
```
